256 devices in a mesh: dev: 256 (over x, z, y, core).
Axes of the slice: x: 4, y: 4, z: 8, core: 2. Of those that a mesh axis runs over, the one named last changes fastest.
Arguments:
- contacts: bfloat16 [2048, 512, 512], P('dev'), as said below
- tile_count: int32 [256], replicated, may hold values from 1 to 8, as said below
- tile_row: int32 [2048], replicated, may hold values from 0 to 511, as said below
- tile_col: int32 [2048], replicated, may hold values from 0 to 511, as said below
- range_rows: int32 [256], replicated, may hold values from 1 to 4, as said below
Outputs:
- bias_one: float32 [256, 2048], P('dev')
- bias_two: float32 [256, 2048], P('dev')
- balanced: bfloat16 [2048, 512, 512], P('dev')
The draws below stay inside these ranges and needn't reach their ends.
Inputs may be any that keep to these rules, and one draw needn't show every extreme that they name: `range_rows`: the ranges sum to 512 tile rows. tile_count[d] is 2 range_rows[d], less one on the last device; device d holds the blocks (r, r) and (r, r + 1) of the rows r of its own range, in its first tile_count[d] slots. `tile_row`: each block (r, r) and (r, r + 1) of the map is held in exactly one slot; slots that are not held have row block 0. `tile_col`: the column block of a held slot is its row block or the next one; slots that are not held have column block 0. `contacts`: entries are positive; a held tile whose row and column blocks are equal is symmetric.
All inputs are finite; a program needn't handle non-finite values.
Results may differ from the reference program's by a relative error of at most 0.001.
Values sent between devices are 32-bit elements; how exact they have to be, the bound alone decides.
No kernel may reach another device: no remote copies, remote signals or barrier semaphores. Data moves between devices by JAX's collectives and lax.ppermute only.
A program may use at most 64 MiB of HBM per device.

```python
import math
import jax
import jax.numpy as jnp
from jax import lax

TILE = 512
TR_DEV = 2
SLOTS = 8
TILE_ROWS = 512
BINS = 262144
RANGE_CAP = 2048
DEVICES = 256


def range_plan(key):
    half = DEVICES // 2
    key_delta = jax.random.fold_in(key, 31)
    key_pick = jax.random.fold_in(key, 32)
    key_other = jax.random.fold_in(key, 33)
    delta = jax.random.randint(key_delta, (half,), 1 - TR_DEV, TR_DEV)
    picked = jax.random.randint(key_pick, (), 0, half)
    other = (picked + 1 + jax.random.randint(key_other, (), 0, half - 1)) % half
    pair_ids = jnp.arange(half)
    first = jnp.where(pair_ids == picked, 2 * TR_DEV, jnp.where(pair_ids == other, TR_DEV - 1, TR_DEV + delta))
    second = jnp.where(pair_ids == picked, 1, jnp.where(pair_ids == other, TR_DEV, TR_DEV - delta))
    return jnp.stack([first, second], 1).reshape(DEVICES).astype(jnp.int32)


def tile_plan(key):
    ranges = range_plan(key)
    counts = 2 * ranges
    counts = counts.at[DEVICES - 1].add(-1)
    row_starts = jnp.cumsum(ranges) - ranges
    slot_ids = jnp.arange(DEVICES * SLOTS)
    owner = slot_ids // SLOTS
    position = slot_ids % SLOTS
    held = position < counts[owner]
    row_blocks = jnp.where(held, row_starts[owner] + position // 2, 0)
    col_blocks = jnp.where(held, row_blocks + position % 2, 0)
    return (counts.astype(jnp.int32), row_blocks.astype(jnp.int32), col_blocks.astype(jnp.int32))


def draw_range_rows(key, part):
    return range_plan(key)


def draw_tile_count(key, part):
    return tile_plan(key)[0]


def draw_tile_row(key, part):
    return tile_plan(key)[1]


def draw_tile_col(key, part):
    return tile_plan(key)[2]


def draw_contacts(key, part):
    counts, row_blocks, col_blocks = tile_plan(key)
    key_entry = jax.random.fold_in(key, 21)
    key_scale = jax.random.fold_in(key, 22)
    total = DEVICES * SLOTS
    entries = jnp.exp(0.4 * jax.random.normal(key_entry, (total, TILE, TILE), jnp.float32))
    spread = math.log(10.0)
    diagonal = (row_blocks == col_blocks)[:, None, None]
    entries = jnp.where(diagonal, 0.5 * (entries + jnp.swapaxes(entries, 1, 2)), entries)
    trend = 1.0 + 2.0 * jnp.arange(BINS).astype(jnp.float32) / BINS
    scales = jnp.exp(jax.random.uniform(key_scale, (BINS,), jnp.float32) * spread) * trend
    row_bins = row_blocks[:, None] * TILE + jnp.arange(TILE)[None, :]
    col_bins = col_blocks[:, None] * TILE + jnp.arange(TILE)[None, :]
    distance = jnp.abs(row_bins[:, :, None] - col_bins[:, None, :]).astype(jnp.float32)
    decay = 1.0 / (1.0 + distance / 64.0)
    values = entries * decay * scales[row_bins][:, :, None] * scales[col_bins][:, None, :]
    return values.astype(jnp.bfloat16)


def setup_inputs(seed: int = 0) -> dict:
    arg_keys = jax.random.split(jax.random.key(seed), 6)
    contacts = draw_contacts(jax.random.fold_in(arg_keys[5], 71), 0)
    tile_count = draw_tile_count(jax.random.fold_in(arg_keys[5], 71), 0)
    tile_row = draw_tile_row(jax.random.fold_in(arg_keys[5], 71), 0)
    tile_col = draw_tile_col(jax.random.fold_in(arg_keys[5], 71), 0)
    range_rows = draw_range_rows(jax.random.fold_in(arg_keys[5], 71), 0)
    return {"contacts": contacts, "tile_count": tile_count, "tile_row": tile_row, "tile_col": tile_col, "range_rows": range_rows}


def reference(contacts, tile_count, tile_row, tile_col, range_rows):
    slot_total = contacts.shape[0]
    slot_count = slot_total // tile_count.shape[0]
    tile_size = contacts.shape[1]
    slot_ids = jnp.arange(slot_total).astype(jnp.int32)
    held_mask = (slot_ids % slot_count < tile_count[slot_ids // slot_count]).astype(jnp.float32)
    offdiag = (tile_row != tile_col).astype(jnp.float32)

    def weighted(inverse, k):
        block = contacts[k].astype(jnp.float32)
        return block * inverse[tile_row[k]][:, None] * inverse[tile_col[k]][None, :]

    def sweep(bias_vec):
        inverse = 1.0 / bias_vec

        def advance(total, k):
            scaled = weighted(inverse, k)
            total = total.at[tile_row[k]].add(jnp.sum(scaled, 1) * held_mask[k])
            total = total.at[tile_col[k]].add(jnp.sum(scaled, 0) * (held_mask[k] * offdiag[k]))
            return total, None

        row_sums, _ = lax.scan(advance, jnp.zeros((TILE_ROWS, tile_size), jnp.float32), slot_ids)
        mean_sum = jnp.sum(row_sums) / BINS
        return bias_vec * (row_sums / mean_sum)

    bias_a = sweep(jnp.ones((TILE_ROWS, tile_size), jnp.float32))
    bias_b = sweep(bias_a)
    inverse_b = 1.0 / bias_b
    balanced = lax.map(lambda k: (weighted(inverse_b, k) * TILE * held_mask[k]).astype(jnp.bfloat16), slot_ids)
    starts = ((jnp.cumsum(range_rows) - range_rows) * tile_size).astype(jnp.int32)
    widths = (range_rows * tile_size).astype(jnp.int32)

    def ranged(bias_vec):
        padded = jnp.concatenate([bias_vec.reshape(-1), jnp.zeros((RANGE_CAP,), jnp.float32)])

        def one_range(first, width):
            piece = lax.dynamic_slice_in_dim(padded, first, RANGE_CAP)
            return jnp.where(jnp.arange(RANGE_CAP).astype(jnp.int32) < width, piece, 0.0)

        return jax.vmap(one_range)(starts, widths)

    return ranged(bias_a), ranged(bias_b), balanced
```

```python
import jax
import jax.numpy as jnp
from jax import lax
from jax.experimental import pallas as pl
from jax.experimental.pallas import tpu as pltpu
from jax.sharding import PartitionSpec as P

TILE = 512
SLOTS = 8
ROWS = 8
CAP = 4
DEVICES = 256
BINS = 262144
F32 = jnp.float32
BF16 = jnp.bfloat16


def iota(shape, axis):
    return lax.broadcasted_iota(jnp.int32, shape, axis)


def row_sums_of(lhs, tile):
    return lax.dot_general(lhs, tile, (((1,), (1,)), ((), ())), preferred_element_type=F32)


def col_sums_of(lhs, tile):
    return lax.dot_general(lhs, tile, (((1,), (0,)), ((), ())), preferred_element_type=F32)


def scatter(by_row, row_at, by_col, col_at):
    out = jnp.zeros((ROWS, TILE), F32)
    rows = iota((ROWS, TILE), 0)
    for j in range(CAP + 1):
        part = jnp.where(row_at == j, by_row, 0.0) + jnp.where(col_at == j, by_col, 0.0)
        out = jnp.where(rows == j, jnp.sum(part, axis=0, keepdims=True), out)
    return out


def gather(window, at):
    out = jnp.zeros((SLOTS, TILE), F32)
    for j in range(CAP + 1):
        out = jnp.where(at == j, window[j : j + 1, :], out)
    return out


def first_kernel(
    c_hbm, count_hbm, row_hbm, col_hbm,
    tiles, sums_ref, spill_ref, first_ref, row_at_ref, col_at_ref, off_at_ref, n_ref,
    count_s, row_s, col_s, tile_sem, int_sem,
):
    ints = [
        pltpu.make_async_copy(count_hbm, count_s, int_sem.at[0]),
        pltpu.make_async_copy(row_hbm, row_s, int_sem.at[1]),
        pltpu.make_async_copy(col_hbm, col_s, int_sem.at[2]),
    ]
    copies = [pltpu.make_async_copy(c_hbm.at[k], tiles.at[k], tile_sem.at[k]) for k in range(SLOTS)]
    for copy in ints:
        copy.start()
    for copy in copies:
        copy.start()
    for copy in ints:
        copy.wait()
    me = lax.axis_index("dev")
    base = me * SLOTS
    count = count_s[me]
    n = (count + 1) // 2
    n_ref[0] = n
    row = [row_s[base + k] for k in range(SLOTS)]
    col = [col_s[base + k] for k in range(SLOTS)]
    start = row[0]
    for k in range(1, SLOTS):
        start = jnp.minimum(start, jnp.where(k < count, row[k], start))
    slots = iota((SLOTS, TILE), 0)
    row_at = jnp.full((SLOTS, TILE), -1, jnp.int32)
    col_at = row_at
    off_at = row_at
    for k in range(SLOTS):
        held = k < count
        local_row = jnp.where(held, row[k] - start, -1)
        local_col = jnp.where(held, col[k] - start, -1)
        local_off = jnp.where(row[k] != col[k], local_col, -1)
        row_at = jnp.where(slots == k, local_row, row_at)
        col_at = jnp.where(slots == k, local_col, col_at)
        off_at = jnp.where(slots == k, local_off, off_at)
    row_at_ref[...] = row_at
    col_at_ref[...] = col_at
    off_at_ref[...] = off_at
    ones = jnp.ones((8, TILE), BF16)
    by_row = jnp.zeros((SLOTS, TILE), F32)
    by_col = by_row
    for k in range(SLOTS):
        copies[k].wait()
        by_row = jnp.where(slots == k, row_sums_of(ones, tiles[k]), by_row)
        by_col = jnp.where(slots == k, col_sums_of(ones, tiles[k]), by_col)
    sums = scatter(by_row, row_at, by_col, off_at)
    sums_ref[...] = sums
    rows = iota((ROWS, TILE), 0)
    first_ref[...] = sums[0:1, :]
    spill_ref[...] = jnp.sum(jnp.where(rows == n, sums, 0.0), axis=0, keepdims=True)


def second_kernel(
    n_ref, tiles, sums_ref, row_at_ref, col_at_ref, off_at_ref, behind_ref, ahead_ref,
    raw_ref, part_ref, scale_ref, spill_ref, first_ref, sent_ref,
):
    n = n_ref[0]
    rows = iota((ROWS, TILE), 0)
    local = sums_ref[...]
    raw = local + jnp.where(rows == 0, behind_ref[...], 0.0) + jnp.where(rows == n, ahead_ref[...], 0.0)
    raw = jnp.where(raw > 0.0, raw, 1.0)
    raw_ref[...] = raw
    own = jnp.where(rows < n, raw, jnp.inf)
    scale = jnp.min(jnp.min(own, axis=0, keepdims=True), axis=1, keepdims=True)
    inverse = scale / raw
    row_at = row_at_ref[...]
    row_inverse = gather(inverse, row_at)
    col_inverse = gather(inverse, col_at_ref[...])
    slots = iota((SLOTS, TILE), 0)

    def halves(x):
        high = x.astype(BF16)
        low = (x - high.astype(F32)).astype(BF16)
        return high, low

    row_high, row_low = halves(row_inverse)
    col_high, col_low = halves(col_inverse)

    def weights(high, low, k):
        return jnp.concatenate(
            [jnp.broadcast_to(high[k : k + 1, :], (8, TILE)), jnp.broadcast_to(low[k : k + 1, :], (8, TILE))], axis=0
        )

    by_row = jnp.zeros((SLOTS, TILE), F32)
    by_col = by_row
    for k in range(SLOTS):
        r = row_sums_of(weights(col_high, col_low, k), tiles[k])
        c = col_sums_of(weights(row_high, row_low, k), tiles[k])
        by_row = jnp.where(slots == k, r[:8] + r[8:], by_row)
        by_col = jnp.where(slots == k, c[:8] + c[8:], by_col)
    part = scatter(by_row * row_inverse, row_at, by_col * col_inverse, off_at_ref[...])
    part_ref[...] = part
    total_one = jnp.sum(jnp.sum(local, axis=0, keepdims=True), axis=1, keepdims=True)
    total_two = jnp.sum(jnp.sum(part, axis=0, keepdims=True), axis=1, keepdims=True)
    sent = jnp.where(iota((1, 128), 1) < 64, total_one, jnp.sqrt(total_two) / scale)
    sent_ref[...] = jnp.broadcast_to(sent, (DEVICES, 128))
    wide = jnp.broadcast_to(scale, (1, 128))
    scale_ref[...] = jnp.broadcast_to(scale, (8, 128))
    first_ref[:, :TILE] = part[0:1, :]
    first_ref[:, TILE:] = wide
    spill_ref[:, :TILE] = jnp.sum(jnp.where(rows == n, part, 0.0), axis=0, keepdims=True)
    spill_ref[:, TILE:] = wide


def factor_kernel(
    n_ref, raw_ref, part_ref, scale_ref, row_at_ref, col_at_ref, behind_ref, ahead_ref,
    weight_ref, row_factor_ref, col_factor_ref,
):
    n = n_ref[0]
    rows = iota((ROWS, TILE), 0)
    scale = jnp.concatenate([scale_ref[0:1, :]] * 4, axis=1)

    def arrived(ref):
        other = jnp.concatenate([ref[:, TILE:]] * 4, axis=1)
        ratio = jnp.where(other > 0.0, scale / jnp.where(other > 0.0, other, 1.0), 0.0)
        return ref[:, :TILE] * ratio * ratio

    part = part_ref[...] + jnp.where(rows == 0, arrived(behind_ref), 0.0) + jnp.where(rows == n, arrived(ahead_ref), 0.0)
    weight = raw_ref[...] / scale * part
    weight = jnp.where(weight > 0.0, weight, 1.0)
    weight_ref[...] = weight
    inverse = 1.0 / weight
    col_factor_ref[...] = gather(inverse, col_at_ref[...])
    upright = jnp.transpose(gather(inverse, row_at_ref[...]))
    for k in range(SLOTS):
        row_factor_ref[k] = jnp.broadcast_to(upright[:, k : k + 1], (TILE, 128))


def last_kernel(
    n_ref, all_ref, c_hbm, raw_ref, weight_ref, scale_ref, row_factor_ref, col_factor_ref,
    one_ref, two_ref, out_hbm, tiles, buffer, in_sem, sem,
):
    copies = [pltpu.make_async_copy(c_hbm.at[k], tiles.at[k], in_sem.at[k]) for k in range(SLOTS)]
    for copy in copies:
        copy.start()
    n = n_ref[0]
    lanes = iota((1, 128), 1)
    everyone = all_ref[...]
    total_one = jnp.sum(everyone, axis=0, keepdims=True)
    mean_one = jnp.sum(jnp.where(lanes == 0, total_one, 0.0), axis=1, keepdims=True) / BINS
    scaled = everyone * mean_one
    total_two = jnp.sum(scaled * scaled, axis=0, keepdims=True)
    mean_two = jnp.sum(jnp.where(lanes == 64, total_two, 0.0), axis=1, keepdims=True) / BINS
    scale = scale_ref[0:1, 0:1]
    unit = scale * mean_two / mean_one
    columns = col_factor_ref[...] * unit * unit * TILE
    for k in range(SLOTS):
        row = jnp.concatenate([row_factor_ref[k]] * 4, axis=1)
        copies[k].wait()
        buffer[k] = (tiles[k].astype(F32) * row * columns[k : k + 1, :]).astype(BF16)
        pltpu.make_async_copy(buffer.at[k], out_hbm.at[k], sem.at[k]).start()
    one = raw_ref[...] / mean_one
    two = weight_ref[...] / unit
    for j in range(CAP):
        one_ref[:, j * TILE : (j + 1) * TILE] = jnp.where(j < n, one[j : j + 1, :], 0.0)
        two_ref[:, j * TILE : (j + 1) * TILE] = jnp.where(j < n, two[j : j + 1, :], 0.0)
    for k in range(SLOTS):
        pltpu.make_async_copy(buffer.at[k], out_hbm.at[k], sem.at[k]).wait()


VMEM = pl.BlockSpec(memory_space=pltpu.VMEM)
SMEM = pl.BlockSpec(memory_space=pltpu.SMEM)
HBM = pl.BlockSpec(memory_space=pltpu.HBM)


def shards(contacts, tile_count, tile_row, tile_col, range_rows):
    forward = [(i, i + 1) for i in range(DEVICES - 1)]
    backward = [(i + 1, i) for i in range(DEVICES - 1)]
    window = pltpu.VMEM((ROWS, TILE), F32)
    index = pltpu.VMEM((SLOTS, TILE), jnp.int32)
    tiles, sums, spill, first, row_at, col_at, off_at, n = pl.pallas_call(
        first_kernel,
        out_shape=(
            pltpu.VMEM((SLOTS, TILE, TILE), BF16), window, pltpu.VMEM((1, TILE), F32), pltpu.VMEM((1, TILE), F32),
            index, index, index, pltpu.SMEM((1,), jnp.int32),
        ),
        in_specs=[HBM] * 4,
        out_specs=(VMEM,) * 7 + (SMEM,),
        scratch_shapes=[
            pltpu.SMEM((DEVICES,), jnp.int32),
            pltpu.SMEM((DEVICES * SLOTS,), jnp.int32),
            pltpu.SMEM((DEVICES * SLOTS,), jnp.int32),
            pltpu.SemaphoreType.DMA((SLOTS,)),
            pltpu.SemaphoreType.DMA((3,)),
        ],
        compiler_params=pltpu.CompilerParams(vmem_limit_bytes=24 << 20),
        name="first",
    )(*(pltpu.with_memory_space_constraint(x, pltpu.HBM) for x in (contacts, tile_count, tile_row, tile_col)))
    behind = lax.ppermute(spill, "dev", forward)
    ahead = lax.ppermute(first, "dev", backward)
    long = pltpu.VMEM((1, TILE + 128), F32)
    raw, part, scale, spill, first, sent = pl.pallas_call(
        second_kernel,
        out_shape=(window, window, pltpu.VMEM((8, 128), F32), long, long, pltpu.VMEM((DEVICES, 128), F32)),
        in_specs=[SMEM] + [VMEM] * 7,
        out_specs=(VMEM,) * 6,
        compiler_params=pltpu.CompilerParams(vmem_limit_bytes=24 << 20),
        name="second",
    )(n, tiles, sums, row_at, col_at, off_at, behind, ahead)
    everyone = lax.all_to_all(sent, "dev", 0, 0, tiled=True)
    behind = lax.ppermute(spill, "dev", forward)
    ahead = lax.ppermute(first, "dev", backward)
    weight, row_factor, col_factor = pl.pallas_call(
        factor_kernel,
        out_shape=(window, pltpu.VMEM((SLOTS, TILE, 128), F32), window),
        in_specs=[SMEM] + [VMEM] * 7,
        out_specs=(VMEM,) * 3,
        compiler_params=pltpu.CompilerParams(vmem_limit_bytes=24 << 20),
        name="factor",
    )(n, raw, part, scale, row_at, col_at, behind, ahead)
    return pl.pallas_call(
        last_kernel,
        out_shape=(
            jax.ShapeDtypeStruct((1, CAP * TILE), F32),
            jax.ShapeDtypeStruct((1, CAP * TILE), F32),
            jax.ShapeDtypeStruct((SLOTS, TILE, TILE), BF16),
        ),
        in_specs=[SMEM, VMEM, HBM] + [VMEM] * 5,
        out_specs=(VMEM, VMEM, HBM),
        scratch_shapes=[pltpu.VMEM((SLOTS, TILE, TILE), BF16)] * 2 + [pltpu.SemaphoreType.DMA((SLOTS,))] * 2,
        compiler_params=pltpu.CompilerParams(vmem_limit_bytes=32 << 20),
        name="last",
    )(n, everyone, pltpu.with_memory_space_constraint(contacts, pltpu.HBM), raw, weight, scale, row_factor, col_factor)


def solution(mesh):
    return jax.shard_map(
        shards,
        mesh=mesh,
        in_specs=(P("dev", None, None), P(), P(), P(), P()),
        out_specs=(P("dev", None), P("dev", None), P("dev", None, None)),
        check_vma=False,
    )
```

```python
import jax
import jax.numpy as jnp
from jax import lax
from jax.experimental import pallas as pl
from jax.experimental.pallas import tpu as pltpu
from jax.sharding import PartitionSpec as P


TILE = 512
SLOTS = 8
ROWS = 8
CAP = 4
EARLY = 4
KEPT = 5
DEVICES = 256
BINS = 262144
F32 = jnp.float32
BF16 = jnp.bfloat16


def iota(shape, axis):
    return lax.broadcasted_iota(jnp.int32, shape, axis)


def row_sums_of(lhs, tile):
    return lax.dot_general(lhs, tile, (((1,), (1,)), ((), ())), preferred_element_type=F32)


def col_sums_of(lhs, tile):
    return lax.dot_general(lhs, tile, (((1,), (0,)), ((), ())), preferred_element_type=F32)


def scatter(by_row, row_at, by_col, col_at):
    out = jnp.zeros((ROWS, TILE), F32)
    rows = iota((ROWS, TILE), 0)
    for j in range(CAP + 1):
        part = jnp.where(row_at == j, by_row, 0.0) + jnp.where(col_at == j, by_col, 0.0)
        out = jnp.where(rows == j, jnp.sum(part, axis=0, keepdims=True), out)
    return out


def gather(window, at):
    out = jnp.zeros((SLOTS, TILE), F32)
    for j in range(CAP + 1):
        out = jnp.where(at == j, window[j : j + 1, :], out)
    return out


def boundary(odd, spill, first):
    return jnp.where(odd, first, spill), jnp.where(odd, spill, first)


def pairs_of(count, off, both, plain):
    for k in range(0, SLOTS, 2):
        usual = jnp.logical_and(off[k] == 0, off[k + 1] != 0)

        @pl.when(jnp.logical_and(k < count, usual))
        def _(k=k):
            plain(k)

        @pl.when(jnp.logical_and(k < count, jnp.logical_not(usual)))
        def _(k=k):
            both(k)


def first_kernel(
    c_hbm, count_hbm, row_hbm, col_hbm,
    tiles, sums_ref, near_ref, far_ref, row_at_ref, col_at_ref, off_at_ref, info_ref,
    count_s, row_s, col_s, by_row_ref, by_col_ref, tile_sem, int_sem,
):
    me = lax.axis_index("dev")
    block = pl.ds(pl.multiple_of((me // 16) * 128, 128), 128)
    ints = [
        pltpu.make_async_copy(count_hbm.at[pl.ds(pl.multiple_of((me // 128) * 128, 128), 128)], count_s, int_sem.at[0]),
        pltpu.make_async_copy(row_hbm.at[block], row_s, int_sem.at[1]),
        pltpu.make_async_copy(col_hbm.at[block], col_s, int_sem.at[2]),
    ]
    copies = [pltpu.make_async_copy(c_hbm.at[k], tiles.at[k], tile_sem.at[k]) for k in range(SLOTS)]
    for copy in ints:
        copy.start()
    for copy in copies[:EARLY]:
        copy.start()
    for copy in ints:
        copy.wait()
    count = count_s[me % 128]
    for k in range(EARLY, SLOTS):

        @pl.when(k - k % 2 < count)
        def _(k=k):
            copies[k].start()

    base = (me % 16) * SLOTS
    n = (count + 1) // 2
    odd = me % 2
    info_ref[0] = n
    info_ref[1] = count
    info_ref[2] = odd
    row = [row_s[base + k] for k in range(SLOTS)]
    col = [col_s[base + k] for k in range(SLOTS)]
    off = [jnp.where(row[k] != col[k], 1, 0) for k in range(SLOTS)]
    off = [jnp.where(k < count, off[k], 1) for k in range(SLOTS)]
    start = row[0]
    for k in range(1, SLOTS):
        start = jnp.minimum(start, jnp.where(k < count, row[k], start))
    slots = iota((SLOTS, TILE), 0)
    row_at = jnp.full((SLOTS, TILE), -1, jnp.int32)
    col_at = row_at
    off_at = row_at
    for k in range(SLOTS):
        info_ref[3 + k] = off[k]
        held = k < count
        local_row = jnp.where(held, row[k] - start, -1)
        local_col = jnp.where(held, col[k] - start, -1)
        local_off = jnp.where(off[k] != 0, local_col, -1)
        row_at = jnp.where(slots == k, local_row, row_at)
        col_at = jnp.where(slots == k, local_col, col_at)
        off_at = jnp.where(slots == k, local_off, off_at)
    row_at_ref[...] = row_at
    col_at_ref[...] = col_at
    off_at_ref[...] = off_at
    ones = jnp.ones((8, TILE), BF16)

    def arrive(k):
        copies[k].wait()
        copies[k + 1].wait()

    def col_of(k):
        total = jnp.sum(tiles[k].astype(F32), axis=0, keepdims=True)
        by_col_ref[k : k + 1, :] = total
        return total

    def plain(k):
        arrive(k)
        by_row_ref[k + 1 : k + 2, :] = row_sums_of(ones, tiles[k + 1])[0:1, :]
        by_row_ref[k : k + 1, :] = col_of(k)
        col_of(k + 1)

    def both(k):
        arrive(k)
        for slot in (k, k + 1):
            by_row_ref[slot : slot + 1, :] = row_sums_of(ones, tiles[slot])[0:1, :]
            col_of(slot)

    pairs_of(count, off, both, plain)
    for k in range(0, EARLY, 2):

        @pl.when(k >= count)
        def _(k=k):
            arrive(k)

    sums = scatter(by_row_ref[...], row_at, by_col_ref[...], off_at)
    sums_ref[...] = sums
    rows = iota((ROWS, TILE), 0)
    spill = jnp.sum(jnp.where(rows == n, sums, 0.0), axis=0, keepdims=True)
    near_ref[...], far_ref[...] = boundary(odd == 1, spill, sums[0:1, :])


def second_kernel(
    info_ref, tiles, sums_ref, row_at_ref, col_at_ref, off_at_ref, near_in, far_in,
    raw_ref, part_ref, scale_ref, near_ref, far_ref, sent_ref,
    by_row_ref, by_col_ref, row_ref, col_ref,
):
    n = info_ref[0]
    count = info_ref[1]
    odd = info_ref[2] == 1
    rows = iota((ROWS, TILE), 0)
    local = sums_ref[...]
    ahead, behind = jnp.where(odd, far_in[...], near_in[...]), jnp.where(odd, near_in[...], far_in[...])
    raw = local + jnp.where(rows == 0, behind, 0.0) + jnp.where(rows == n, ahead, 0.0)
    raw = jnp.where(raw > 0.0, raw, 1.0)
    raw_ref[...] = raw
    own = jnp.where(rows < n, raw, jnp.inf)
    scale = jnp.min(jnp.min(own, axis=0, keepdims=True), axis=1, keepdims=True)
    inverse = scale / raw
    row_at = row_at_ref[...]
    row_inverse = gather(inverse, row_at)
    col_inverse = gather(inverse, col_at_ref[...])
    row_ref[...] = row_inverse
    col_ref[...] = col_inverse

    def weights(ref, k):
        x = jnp.broadcast_to(ref[k : k + 1, :], (8, TILE))
        high = x.astype(BF16)
        low = (x - high.astype(F32)).astype(BF16)
        return jnp.concatenate([high, low], axis=0)

    def row_of(k):
        r = row_sums_of(weights(col_ref, k), tiles[k])
        by_row_ref[k : k + 1, :] = r[0:1, :] + r[8:9, :]

    def col_of(k):
        c = col_sums_of(weights(row_ref, k), tiles[k])
        by_col_ref[k : k + 1, :] = c[0:1, :] + c[8:9, :]

    def plain(k):
        row_of(k + 1)
        row_of(k)
        col_of(k + 1)

    def both(k):
        for slot in (k, k + 1):
            row_of(slot)
            col_of(slot)

    pairs_of(count, [info_ref[3 + k] for k in range(SLOTS)], both, plain)
    part = scatter(by_row_ref[...] * row_inverse, row_at, by_col_ref[...] * col_inverse, off_at_ref[...])
    part_ref[...] = part
    total_one = jnp.sum(jnp.sum(local, axis=0, keepdims=True), axis=1, keepdims=True)
    total_two = jnp.sum(jnp.sum(part, axis=0, keepdims=True), axis=1, keepdims=True)
    sent = jnp.where(iota((1, 128), 1) < 64, total_one, jnp.sqrt(total_two) / scale)
    sent_ref[...] = jnp.broadcast_to(sent, (DEVICES, 128))
    wide = jnp.broadcast_to(scale, (1, 128))
    scale_ref[...] = jnp.broadcast_to(scale, (8, 128))
    spill = jnp.sum(jnp.where(rows == n, part, 0.0), axis=0, keepdims=True)
    near_ref[:, :TILE], far_ref[:, :TILE] = boundary(odd, spill, part[0:1, :])
    near_ref[:, TILE:] = wide
    far_ref[:, TILE:] = wide


def factor_kernel(
    info_ref, c_hbm, raw_ref, part_ref, scale_ref, row_at_ref, col_at_ref, near_in, far_in,
    tiles, weight_ref, row_factor_ref, col_factor_ref, sem,
):
    copy = pltpu.make_async_copy(c_hbm.at[pl.ds(0, KEPT)], tiles, sem)
    copy.start()
    n = info_ref[0]
    odd = info_ref[2] == 1
    rows = iota((ROWS, TILE), 0)
    scale = jnp.concatenate([scale_ref[0:1, :]] * 4, axis=1)
    ahead = jnp.where(odd, far_in[...], near_in[...])
    behind = jnp.where(odd, near_in[...], far_in[...])

    def rescaled(x):
        other = jnp.concatenate([x[:, TILE:]] * 4, axis=1)
        ratio = jnp.where(other > 0.0, scale / jnp.where(other > 0.0, other, 1.0), 0.0)
        return x[:, :TILE] * ratio * ratio

    part = part_ref[...] + jnp.where(rows == 0, rescaled(behind), 0.0) + jnp.where(rows == n, rescaled(ahead), 0.0)
    weight = raw_ref[...] / scale * part
    weight = jnp.where(weight > 0.0, weight, 1.0)
    weight_ref[...] = weight
    inverse = 1.0 / weight
    col_factor_ref[...] = gather(inverse, col_at_ref[...])
    row_factor_ref[...] = jnp.transpose(gather(inverse, row_at_ref[...]))
    copy.wait()


def last_kernel(
    info_ref, all_ref, c_hbm, kept, raw_ref, weight_ref, scale_ref, row_factor_ref, col_factor_ref,
    one_ref, two_ref, out_hbm, tiles, buffer, zeros, columns_ref, in_sem, sem,
):
    n = info_ref[0]
    count = info_ref[1]
    copies = [pltpu.make_async_copy(c_hbm.at[k], tiles.at[k - KEPT], in_sem.at[k - KEPT]) for k in range(KEPT, SLOTS)]
    for k in range(KEPT, SLOTS):

        @pl.when(k < count)
        def _(k=k):
            copies[k - KEPT].start()

    zeros[...] = jnp.zeros((TILE, TILE), BF16)
    for k in range(1, SLOTS):

        @pl.when(k >= count)
        def _(k=k):
            pltpu.make_async_copy(zeros, out_hbm.at[k], sem.at[k]).start()

    lanes = iota((1, 128), 1)
    everyone = all_ref[...]
    total_one = jnp.sum(everyone, axis=0, keepdims=True)
    mean_one = jnp.sum(jnp.where(lanes == 0, total_one, 0.0), axis=1, keepdims=True) / BINS
    scaled = everyone * mean_one
    total_two = jnp.sum(scaled * scaled, axis=0, keepdims=True)
    mean_two = jnp.sum(jnp.where(lanes == 64, total_two, 0.0), axis=1, keepdims=True) / BINS
    scale = scale_ref[0:1, 0:1]
    unit = scale * mean_two / mean_one
    columns_ref[...] = col_factor_ref[...] * unit * unit * TILE
    for k in range(SLOTS):

        @pl.when(k < count)
        def _(k=k):
            if k >= KEPT:
                copies[k - KEPT].wait()
                tile = tiles[k - KEPT]
            else:
                tile = kept[k]
            row = jnp.broadcast_to(row_factor_ref[:, k : k + 1], (TILE, TILE))
            buffer[k] = (tile.astype(F32) * row * columns_ref[k : k + 1, :]).astype(BF16)
            pltpu.make_async_copy(buffer.at[k], out_hbm.at[k], sem.at[k]).start()

    one = raw_ref[...] / mean_one
    two = weight_ref[...] / unit
    for j in range(CAP):
        one_ref[:, j * TILE : (j + 1) * TILE] = jnp.where(j < n, one[j : j + 1, :], 0.0)
        two_ref[:, j * TILE : (j + 1) * TILE] = jnp.where(j < n, two[j : j + 1, :], 0.0)
    for k in range(SLOTS):
        pltpu.make_async_copy(buffer.at[k], out_hbm.at[k], sem.at[k]).wait()


VMEM = pl.BlockSpec(memory_space=pltpu.VMEM)
SMEM = pl.BlockSpec(memory_space=pltpu.SMEM)
HBM = pl.BlockSpec(memory_space=pltpu.HBM)


def in_hbm(x):
    return pltpu.with_memory_space_constraint(x, pltpu.HBM)


def shards(contacts, tile_count, tile_row, tile_col, range_rows):
    near_pairs = [(i, i ^ 1) for i in range(DEVICES)]
    far_pairs = [(i, ((i + 1) ^ 1) - 1) for i in range(1, DEVICES - 1)]
    window = pltpu.VMEM((ROWS, TILE), F32)
    index = pltpu.VMEM((SLOTS, TILE), jnp.int32)
    line = pltpu.VMEM((1, TILE), F32)
    long = pltpu.VMEM((1, TILE + 128), F32)
    tiles, sums, near, far, row_at, col_at, off_at, info = pl.pallas_call(
        first_kernel,
        out_shape=(
            pltpu.VMEM((SLOTS, TILE, TILE), BF16), window, line, line, index, index, index, pltpu.SMEM((11,), jnp.int32),
        ),
        in_specs=[HBM] * 4,
        out_specs=(VMEM,) * 7 + (SMEM,),
        scratch_shapes=[
            pltpu.SMEM((128,), jnp.int32),
            pltpu.SMEM((128,), jnp.int32),
            pltpu.SMEM((128,), jnp.int32),
            window,
            window,
            pltpu.SemaphoreType.DMA((SLOTS,)),
            pltpu.SemaphoreType.DMA((3,)),
        ],
        compiler_params=pltpu.CompilerParams(vmem_limit_bytes=24 << 20),
        name="first",
    )(*(in_hbm(x) for x in (contacts, tile_count, tile_row, tile_col)))
    far = lax.ppermute(far, "dev", far_pairs)
    near = lax.ppermute(near, "dev", near_pairs)
    raw, part, scale, near, far, sent = pl.pallas_call(
        second_kernel,
        out_shape=(window, window, pltpu.VMEM((8, 128), F32), long, long, pltpu.VMEM((DEVICES, 128), F32)),
        in_specs=[SMEM] + [VMEM] * 7,
        out_specs=(VMEM,) * 6,
        scratch_shapes=[window] * 4,
        compiler_params=pltpu.CompilerParams(vmem_limit_bytes=24 << 20),
        name="second",
    )(info, tiles, sums, row_at, col_at, off_at, near, far)
    far = lax.ppermute(far, "dev", far_pairs)
    near = lax.ppermute(near, "dev", near_pairs)
    everyone = lax.all_to_all(sent, "dev", 0, 0, tiled=True)
    tiles, weight, row_factor, col_factor = pl.pallas_call(
        factor_kernel,
        out_shape=(pltpu.VMEM((KEPT, TILE, TILE), BF16), window, pltpu.VMEM((TILE, SLOTS), F32), window),
        in_specs=[SMEM, HBM] + [VMEM] * 7,
        out_specs=(VMEM,) * 4,
        scratch_shapes=[pltpu.SemaphoreType.DMA],
        compiler_params=pltpu.CompilerParams(vmem_limit_bytes=24 << 20),
        name="factor",
    )(info, in_hbm(contacts), raw, part, scale, row_at, col_at, near, far)
    return pl.pallas_call(
        last_kernel,
        out_shape=(
            jax.ShapeDtypeStruct((1, CAP * TILE), F32),
            jax.ShapeDtypeStruct((1, CAP * TILE), F32),
            jax.ShapeDtypeStruct((SLOTS, TILE, TILE), BF16),
        ),
        in_specs=[SMEM, VMEM, HBM] + [VMEM] * 6,
        out_specs=(VMEM, VMEM, HBM),
        scratch_shapes=[
            pltpu.VMEM((SLOTS - KEPT, TILE, TILE), BF16),
            pltpu.VMEM((SLOTS, TILE, TILE), BF16),
            pltpu.VMEM((TILE, TILE), BF16),
            window,
            pltpu.SemaphoreType.DMA((SLOTS - KEPT,)),
            pltpu.SemaphoreType.DMA((SLOTS,)),
        ],
        compiler_params=pltpu.CompilerParams(vmem_limit_bytes=32 << 20),
        name="last",
    )(info, everyone, in_hbm(contacts), tiles, raw, weight, scale, row_factor, col_factor)


def solution(mesh):
    return jax.shard_map(
        shards,
        mesh=mesh,
        in_specs=(P("dev", None, None), P(), P(), P(), P()),
        out_specs=(P("dev", None), P("dev", None), P("dev", None, None)),
        check_vma=False,
    )
```

```python
import jax
import jax.numpy as jnp
from jax import lax
from jax.experimental import pallas as pl
from jax.experimental.pallas import tpu as pltpu
from jax.sharding import PartitionSpec as P


TILE = 512
SLOTS = 8
ROWS = 8
CAP = 4
EARLY = 4
KEPT = 5
DEVICES = 256
BINS = 262144
AT_ROW, AT_COL, AT_DIAG, AT_OFF, INFO = 3, 11, 19, 23, 27
F32 = jnp.float32
BF16 = jnp.bfloat16


def iota(shape, axis):
    return lax.broadcasted_iota(jnp.int32, shape, axis)


def row_sums_of(lhs, tile):
    return lax.dot_general(lhs, tile, (((1,), (1,)), ((), ())), preferred_element_type=F32)


def col_sums_of(lhs, tile):
    return lax.dot_general(lhs, tile, (((1,), (0,)), ((), ())), preferred_element_type=F32)


def boundary(odd, spill, first):
    return jnp.where(odd, first, spill), jnp.where(odd, spill, first)


def gather(window, at):
    out = jnp.zeros((SLOTS, TILE), F32)
    for j in range(CAP + 1):
        out = jnp.where(at == j, window[j : j + 1, :], out)
    return out


def upright_sum(tile):
    return jnp.sum(tile.astype(F32), axis=0, keepdims=True)


def level_sum(tile):
    return row_sums_of(jnp.ones((8, TILE), BF16), tile)[0:1, :]


def weights(line):
    x = jnp.broadcast_to(line, (8, TILE))
    high = x.astype(BF16)
    low = (x - high.astype(F32)).astype(BF16)
    return jnp.concatenate([high, low], axis=0)


def level(tile, line):
    out = row_sums_of(weights(line), tile)
    return out[0:1, :] + out[8:9, :]


def upright(tile, line):
    out = col_sums_of(weights(line), tile)
    return out[0:1, :] + out[8:9, :]


def edge_kernel(
    c_hbm, count_hbm, row_hbm, col_hbm,
    edge, diagonal, near_ref, far_ref, first_ref, spill_ref, info_ref,
    count_s, row_s, col_s, tile_sem, int_sem,
):
    me = lax.axis_index("dev")
    block = pl.ds(pl.multiple_of((me // 16) * 128, 128), 128)
    ints = [
        pltpu.make_async_copy(count_hbm.at[pl.ds(pl.multiple_of((me // 128) * 128, 128), 128)], count_s, int_sem.at[0]),
        pltpu.make_async_copy(row_hbm.at[block], row_s, int_sem.at[1]),
        pltpu.make_async_copy(col_hbm.at[block], col_s, int_sem.at[2]),
    ]
    copies = [pltpu.make_async_copy(c_hbm.at[max(2 * j - 1, 0)], edge.at[j], tile_sem.at[j]) for j in range(CAP + 1)]
    other = pltpu.make_async_copy(c_hbm.at[2], diagonal, tile_sem.at[CAP + 1])
    for copy in ints:
        copy.start()
    for copy in copies[:EARLY]:
        copy.start()
    other.start()
    for copy in ints:
        copy.wait()
    count = count_s[me % 128]
    for j in range(EARLY, CAP + 1):

        @pl.when(2 * j - 1 < count)
        def _(j=j):
            copies[j].start()

    base = (me % 16) * SLOTS
    n = (count + 1) // 2
    odd = me % 2
    row = [row_s[base + k] for k in range(SLOTS)]
    col = [col_s[base + k] for k in range(SLOTS)]
    start = row[0]
    for k in range(1, SLOTS):
        start = jnp.minimum(start, jnp.where(k < count, row[k], start))
    info_ref[0] = n
    info_ref[1] = count
    info_ref[2] = odd
    for j in range(2 * CAP):
        info_ref[AT_DIAG + j] = 0
    strange = jnp.int32(0)
    for k in range(SLOTS):
        held = k < count
        local_row = jnp.where(held, row[k] - start, -1)
        local_col = jnp.where(held, col[k] - start, -1)
        info_ref[AT_ROW + k] = local_row
        info_ref[AT_COL + k] = local_col
        usual = jnp.logical_and(local_row == k // 2, local_col == (k + 1) // 2)
        strange = jnp.where(jnp.logical_or(usual, jnp.logical_not(held)), strange, 1)

        @pl.when(held)
        def _(k=k, local_row=local_row, local_col=local_col):
            info_ref[jnp.where(local_row == local_col, AT_DIAG, AT_OFF) + local_row] = k

    for copy in copies[:EARLY]:
        copy.wait()
    for j in range(EARLY, CAP + 1):

        @pl.when(2 * j - 1 < count)
        def _(j=j):
            copies[j].wait()

    @pl.when(strange != 0)
    def _():
        for j in range(CAP + 1):
            slot = info_ref[AT_DIAG] if j == 0 else info_ref[AT_OFF + j - 1]
            copy = pltpu.make_async_copy(c_hbm.at[slot], edge.at[j], tile_sem.at[j])
            copy.start()
            copy.wait()

    def rest():
        other.wait()

        @pl.when(strange != 0)
        def _():
            copy = pltpu.make_async_copy(c_hbm.at[info_ref[AT_DIAG + 1]], diagonal, tile_sem.at[CAP + 1])
            copy.start()
            copy.wait()

    first = upright_sum(edge[0]) + jnp.where(count >= 2, level_sum(edge[1]), 0.0)
    spill = jnp.where(count == 2 * n, upright_sum(edge[n]), 0.0)
    first_ref[...] = first
    spill_ref[...] = spill
    near_ref[...], far_ref[...] = boundary(odd == 1, spill, first)
    rest()


def middle_kernel(
    info_ref, c_hbm, edge, one_diagonal, first_ref, spill_ref,
    sums_ref, grown_ref, scale_ref,
    more_diagonals, inverse_ref, sem,
):
    n = info_ref[0]
    count = info_ref[1]
    last = count == 2 * n
    copies = [
        pltpu.make_async_copy(c_hbm.at[info_ref[AT_DIAG + j]], more_diagonals.at[j - 2], sem.at[j - 2])
        for j in range(2, CAP)
    ]
    for j in range(2, CAP):

        @pl.when(j < n)
        def _(j=j):
            copies[j - 2].start()

    def diagonal(j):
        return one_diagonal[...] if j == 1 else more_diagonals[j - 2]

    sums_ref[...] = jnp.zeros((ROWS, TILE), F32)
    grown_ref[...] = jnp.zeros((ROWS, TILE), F32)
    sums_ref[0:1, :] = first_ref[...]
    sums_ref[pl.ds(n, 1), :] = spill_ref[...]
    for j in range(1, CAP):

        @pl.when(j < n)
        def _(j=j):
            above = upright_sum(edge[j])
            across = jnp.where(jnp.logical_or(j + 1 < n, last), level_sum(edge[j + 1]), 0.0)
            if j > 1:
                copies[j - 2].wait()
            sums_ref[j : j + 1, :] = above + across + upright_sum(diagonal(j))

    sums = sums_ref[...]
    rows = iota((ROWS, TILE), 0)
    own = jnp.where(jnp.logical_and(rows < n, sums > 0.0), sums, jnp.inf)
    scale = jnp.min(jnp.min(own, axis=0, keepdims=True), axis=1, keepdims=True)
    total = jnp.sum(jnp.sum(sums, axis=0, keepdims=True), axis=1, keepdims=True)
    scale_ref[...] = jnp.where(iota((8, 128), 0) == 0, scale, total)
    inverse_ref[...] = scale / jnp.where(sums > 0.0, sums, 1.0)
    for j in range(1, CAP):

        @pl.when(j < n)
        def _(j=j):
            line = inverse_ref[j : j + 1, :]
            grown_ref[j - 1 : j, :] += level(edge[j], line)
            grown_ref[j : j + 1, :] += level(diagonal(j), line)
            below = upright(edge[j + 1], line)
            grown_ref[j + 1 : j + 2, :] += jnp.where(jnp.logical_or(j + 1 < n, last), below, 0.0)


def second_kernel(
    info_ref, edge, sums_ref, grown_ref, scale_in, near_in, far_in,
    raw_ref, part_ref, near_ref, far_ref, sent_ref,
    inverse_ref,
):
    n = info_ref[0]
    count = info_ref[1]
    odd = info_ref[2] == 1
    rows = iota((ROWS, TILE), 0)
    local = sums_ref[...]
    ahead, behind = jnp.where(odd, far_in[...], near_in[...]), jnp.where(odd, near_in[...], far_in[...])
    raw = local + jnp.where(rows == 0, behind, 0.0) + jnp.where(rows == n, ahead, 0.0)
    raw = jnp.where(raw > 0.0, raw, 1.0)
    raw_ref[...] = raw
    scale = scale_in[0:1, 0:1]
    inverse = scale / raw
    inverse_ref[...] = inverse
    top = inverse_ref[0:1, :]
    next_row = inverse_ref[pl.ds(n, 1), :]
    here = level(edge[0], top)
    below = jnp.where(count >= 2, upright(edge[1], top), 0.0)
    across = jnp.where(count == 2 * n, level(edge[n], next_row), 0.0)
    grown = grown_ref[...] + jnp.where(rows == 0, here, 0.0) + jnp.where(rows == 1, below, 0.0)
    part = (grown + jnp.where(rows == n - 1, across, 0.0)) * inverse
    part_ref[...] = part
    column = jnp.sum(part, axis=0, keepdims=True)
    quarter = column[:, :128] + column[:, 128:256] + column[:, 256:384] + column[:, 384:]
    folded = jnp.broadcast_to(quarter, (8, 128))
    folded = folded + pltpu.roll(folded, 64, 1)
    sent = jnp.where(iota((8, 128), 1) < 64, scale_in[1:2, :], jnp.sqrt(folded) / scale_in[0:1, :])
    sent_ref[...] = jnp.concatenate([sent] * (DEVICES // 8), axis=0)
    spill = jnp.sum(jnp.where(rows == n, part, 0.0), axis=0, keepdims=True)
    near_ref[:, :TILE], far_ref[:, :TILE] = boundary(odd, spill, part[0:1, :])
    near_ref[:, TILE:] = scale_in[0:1, :]
    far_ref[:, TILE:] = scale_in[0:1, :]


def factor_kernel(
    info_ref, c_hbm, raw_ref, part_ref, scale_ref, near_in, far_in,
    tiles, weight_ref, row_factor_ref, col_factor_ref, out_hbm, zeros, sem, zero_sem,
):
    copy = pltpu.make_async_copy(c_hbm.at[pl.ds(0, KEPT)], tiles, sem)
    copy.start()
    n = info_ref[0]
    count = info_ref[1]
    zeros[...] = jnp.zeros((TILE, TILE), BF16)
    blanks = [None] + [pltpu.make_async_copy(zeros, out_hbm.at[k], zero_sem.at[k]) for k in range(1, SLOTS)]
    for k in range(1, SLOTS):

        @pl.when(k >= count)
        def _(k=k):
            blanks[k].start()

    odd = info_ref[2] == 1
    rows = iota((ROWS, TILE), 0)
    scale = jnp.concatenate([scale_ref[0:1, :]] * 4, axis=1)
    ahead = jnp.where(odd, far_in[...], near_in[...])
    behind = jnp.where(odd, near_in[...], far_in[...])

    def rescaled(x):
        other = jnp.concatenate([x[:, TILE:]] * 4, axis=1)
        ratio = jnp.where(other > 0.0, scale / jnp.where(other > 0.0, other, 1.0), 0.0)
        return x[:, :TILE] * ratio * ratio

    part = part_ref[...] + jnp.where(rows == 0, rescaled(behind), 0.0) + jnp.where(rows == n, rescaled(ahead), 0.0)
    weight = raw_ref[...] / scale * part
    weight = jnp.where(weight > 0.0, weight, 1.0)
    weight_ref[...] = weight
    inverse = 1.0 / weight
    slots = iota((SLOTS, TILE), 0)
    col_at = jnp.full((SLOTS, TILE), -1, jnp.int32)
    for k in range(SLOTS):
        col_at = jnp.where(slots == k, info_ref[AT_COL + k], col_at)
    col_factor_ref[...] = gather(inverse, col_at)
    row_factor_ref[...] = jnp.transpose(inverse)
    copy.wait()
    for k in range(1, SLOTS):

        @pl.when(k >= count)
        def _(k=k):
            blanks[k].wait()


def last_kernel(
    info_ref, all_ref, c_hbm, kept, raw_ref, weight_ref, scale_ref, row_factor_ref, col_factor_ref, blank_hbm,
    one_hbm, two_hbm, out_hbm, tiles, buffer, one_ref, two_ref, columns_ref, rows_ref, in_sem, sem, bias_sem,
):
    n = info_ref[0]
    count = info_ref[1]
    copies = [pltpu.make_async_copy(c_hbm.at[k], tiles.at[k - KEPT], in_sem.at[k - KEPT]) for k in range(KEPT, SLOTS)]
    for k in range(KEPT, SLOTS):

        @pl.when(k < count)
        def _(k=k):
            copies[k - KEPT].start()

    for j in range(CAP):
        rows_ref[j] = jnp.broadcast_to(row_factor_ref[:, j : j + 1], (TILE, 128))
    lanes = iota((1, 128), 1)
    everyone = all_ref[...]
    total_one = jnp.sum(everyone, axis=0, keepdims=True)
    mean_one = jnp.sum(jnp.where(lanes == 0, total_one, 0.0), axis=1, keepdims=True) / BINS
    scaled = everyone * mean_one
    total_two = jnp.sum(scaled * scaled, axis=0, keepdims=True)
    mean_two = jnp.sum(jnp.where(lanes >= 64, total_two, 0.0), axis=1, keepdims=True) / BINS
    scale = scale_ref[0:1, 0:1]
    unit = scale * mean_two / mean_one
    columns_ref[...] = col_factor_ref[...] * unit * unit * TILE
    one = raw_ref[...] / mean_one
    two = weight_ref[...] / unit
    for j in range(CAP):
        one_ref[:, j * TILE : (j + 1) * TILE] = jnp.where(j < n, one[j : j + 1, :], 0.0)
        two_ref[:, j * TILE : (j + 1) * TILE] = jnp.where(j < n, two[j : j + 1, :], 0.0)
    biases = [
        pltpu.make_async_copy(one_ref, one_hbm, bias_sem.at[0]),
        pltpu.make_async_copy(two_ref, two_hbm, bias_sem.at[1]),
    ]
    for copy in biases:
        copy.start()
    for k in range(SLOTS):

        @pl.when(k < count)
        def _(k=k):
            if k >= KEPT:
                copies[k - KEPT].wait()
                tile = tiles[k - KEPT]
            else:
                tile = kept[k]
            row = jnp.concatenate([rows_ref[info_ref[AT_ROW + k]]] * 4, axis=1)
            buffer[k] = (tile.astype(F32) * row * columns_ref[k : k + 1, :]).astype(BF16)
            pltpu.make_async_copy(buffer.at[k], out_hbm.at[k], sem.at[k]).start()

    for copy in biases:
        copy.wait()
    for k in range(SLOTS):

        @pl.when(k < count)
        def _(k=k):
            pltpu.make_async_copy(buffer.at[k], out_hbm.at[k], sem.at[k]).wait()


VMEM = pl.BlockSpec(memory_space=pltpu.VMEM)
SMEM = pl.BlockSpec(memory_space=pltpu.SMEM)
HBM = pl.BlockSpec(memory_space=pltpu.HBM)


def in_hbm(x):
    return pltpu.with_memory_space_constraint(x, pltpu.HBM)


def shards(contacts, tile_count, tile_row, tile_col, range_rows):
    near_pairs = [(i, i ^ 1) for i in range(DEVICES)]
    far_pairs = [(i, ((i + 1) ^ 1) - 1) for i in range(1, DEVICES - 1)]
    window = pltpu.VMEM((ROWS, TILE), F32)
    line = pltpu.VMEM((1, TILE), F32)
    long = pltpu.VMEM((1, TILE + 128), F32)
    splat = pltpu.VMEM((8, 128), F32)
    edge, diagonal, near, far, first, spill, info = pl.pallas_call(
        edge_kernel,
        out_shape=(
            pltpu.VMEM((CAP + 1, TILE, TILE), BF16), pltpu.VMEM((TILE, TILE), BF16), line, line, line, line,
            pltpu.SMEM((INFO,), jnp.int32),
        ),
        in_specs=[HBM] * 4,
        out_specs=(VMEM,) * 6 + (SMEM,),
        scratch_shapes=[
            pltpu.SMEM((128,), jnp.int32),
            pltpu.SMEM((128,), jnp.int32),
            pltpu.SMEM((128,), jnp.int32),
            pltpu.SemaphoreType.DMA((CAP + 2,)),
            pltpu.SemaphoreType.DMA((3,)),
        ],
        compiler_params=pltpu.CompilerParams(vmem_limit_bytes=24 << 20),
        name="edge",
    )(*(in_hbm(x) for x in (contacts, tile_count, tile_row, tile_col)))
    far = lax.ppermute(far, "dev", far_pairs)
    near = lax.ppermute(near, "dev", near_pairs)
    sums, grown, scale = pl.pallas_call(
        middle_kernel,
        out_shape=(window, window, splat),
        in_specs=[SMEM, HBM] + [VMEM] * 4,
        out_specs=(VMEM,) * 3,
        scratch_shapes=[
            pltpu.VMEM((CAP - 2, TILE, TILE), BF16),
            window,
            pltpu.SemaphoreType.DMA((CAP - 2,)),
        ],
        compiler_params=pltpu.CompilerParams(vmem_limit_bytes=24 << 20),
        name="middle",
    )(info, in_hbm(contacts), edge, diagonal, first, spill)
    raw, part, near, far, sent = pl.pallas_call(
        second_kernel,
        out_shape=(window, window, long, long, pltpu.VMEM((DEVICES, 128), F32)),
        in_specs=[SMEM] + [VMEM] * 6,
        out_specs=(VMEM,) * 5,
        scratch_shapes=[window],
        compiler_params=pltpu.CompilerParams(vmem_limit_bytes=24 << 20),
        name="second",
    )(info, edge, sums, grown, scale, near, far)
    far = lax.ppermute(far, "dev", far_pairs)
    near = lax.ppermute(near, "dev", near_pairs)
    everyone = lax.all_to_all(sent, "dev", 0, 0, tiled=True)
    balanced = jax.ShapeDtypeStruct((SLOTS, TILE, TILE), BF16)
    tiles, weight, row_factor, col_factor, blank = pl.pallas_call(
        factor_kernel,
        out_shape=(pltpu.VMEM((KEPT, TILE, TILE), BF16), window, pltpu.VMEM((TILE, SLOTS), F32), window, balanced),
        in_specs=[SMEM, HBM] + [VMEM] * 5,
        out_specs=(VMEM,) * 4 + (HBM,),
        scratch_shapes=[
            pltpu.VMEM((TILE, TILE), BF16), pltpu.SemaphoreType.DMA, pltpu.SemaphoreType.DMA((SLOTS,)),
        ],
        compiler_params=pltpu.CompilerParams(vmem_limit_bytes=24 << 20),
        name="factor",
    )(info, in_hbm(contacts), raw, part, scale, near, far)
    return pl.pallas_call(
        last_kernel,
        out_shape=(
            jax.ShapeDtypeStruct((1, CAP * TILE), F32),
            jax.ShapeDtypeStruct((1, CAP * TILE), F32),
            balanced,
        ),
        in_specs=[SMEM, VMEM, HBM] + [VMEM] * 6 + [HBM],
        out_specs=(HBM,) * 3,
        input_output_aliases={9: 2},
        scratch_shapes=[
            pltpu.VMEM((SLOTS - KEPT, TILE, TILE), BF16),
            pltpu.VMEM((SLOTS, TILE, TILE), BF16),
            pltpu.VMEM((1, CAP * TILE), F32),
            pltpu.VMEM((1, CAP * TILE), F32),
            window,
            pltpu.VMEM((CAP, TILE, 128), F32),
            pltpu.SemaphoreType.DMA((SLOTS - KEPT,)),
            pltpu.SemaphoreType.DMA((SLOTS,)),
            pltpu.SemaphoreType.DMA((2,)),
        ],
        compiler_params=pltpu.CompilerParams(vmem_limit_bytes=32 << 20),
        name="last",
    )(info, everyone, in_hbm(contacts), tiles, raw, weight, scale, row_factor, col_factor, blank)


def solution(mesh):
    return jax.shard_map(
        shards,
        mesh=mesh,
        in_specs=(P("dev", None, None), P(), P(), P(), P()),
        out_specs=(P("dev", None), P("dev", None), P("dev", None, None)),
        check_vma=False,
    )
```

```python
import jax
import jax.numpy as jnp
from jax import lax
from jax.experimental import pallas as pl
from jax.experimental.pallas import tpu as pltpu
from jax.sharding import PartitionSpec as P


TILE = 512
SLOTS = 8
ROWS = 8
CAP = 4
EARLY = 4
HALVES = 1
KEPT = 5
DEVICES = 256
BINS = 262144
AT_ROW, AT_COL, AT_DIAG, AT_OFF, EARLY_BIRD, STRANGE, INFO = 3, 11, 19, 23, 27, 28, 29
F32 = jnp.float32
BF16 = jnp.bfloat16


def iota(shape, axis):
    return lax.broadcasted_iota(jnp.int32, shape, axis)


def row_sums_of(lhs, tile):
    return lax.dot_general(lhs, tile, (((1,), (1,)), ((), ())), preferred_element_type=F32)


def col_sums_of(lhs, tile):
    return lax.dot_general(lhs, tile, (((1,), (0,)), ((), ())), preferred_element_type=F32)


def boundary(odd, spill, first):
    return jnp.where(odd, first, spill), jnp.where(odd, spill, first)


def gather(window, at):
    out = jnp.zeros((SLOTS, TILE), F32)
    for j in range(CAP + 1):
        out = jnp.where(at == j, window[j : j + 1, :], out)
    return out


def upright_sum(tile):
    return jnp.sum(tile.astype(F32), axis=0, keepdims=True)


def level_sum(tile):
    return row_sums_of(jnp.ones((8, TILE), BF16), tile)[0:1, :]


def weights(line):
    x = jnp.broadcast_to(line, (8, TILE))
    high = x.astype(BF16)
    low = (x - high.astype(F32)).astype(BF16)
    return jnp.concatenate([high, low], axis=0)


def level(tile, line):
    out = row_sums_of(weights(line), tile)
    return out[0:1, :] + out[8:9, :]


def upright(tile, line):
    out = col_sums_of(weights(line), tile)
    return out[0:1, :] + out[8:9, :]


def interior(
    info_ref, c_hbm, edge, diagonals, first_ref, spill_ref,
    sums_ref, grown_ref, scale_ref,
    last_diagonal, inverse_ref, sem,
):
    n = info_ref[0]
    count = info_ref[1]
    last = count == 2 * n
    copy = pltpu.make_async_copy(c_hbm.at[info_ref[AT_DIAG + CAP - 1]], last_diagonal, sem)

    @pl.when(n == CAP)
    def _():
        copy.start()

    def diagonal(j):
        return last_diagonal[...] if j == CAP - 1 else diagonals[j - 1]

    sums_ref[...] = jnp.zeros((ROWS, TILE), F32)
    grown_ref[...] = jnp.zeros((ROWS, TILE), F32)
    sums_ref[0:1, :] = first_ref[...]
    sums_ref[pl.ds(n, 1), :] = spill_ref[...]
    for j in range(1, CAP):

        @pl.when(j < n)
        def _(j=j):
            above = upright_sum(edge[j])
            across = jnp.where(jnp.logical_or(j + 1 < n, last), level_sum(edge[j + 1]), 0.0)
            if j == CAP - 1:
                copy.wait()
            sums_ref[j : j + 1, :] = above + across + upright_sum(diagonal(j))

    sums = sums_ref[...]
    rows = iota((ROWS, TILE), 0)
    own = jnp.where(jnp.logical_and(rows < n, sums > 0.0), sums, jnp.inf)
    scale = jnp.min(jnp.min(own, axis=0, keepdims=True), axis=1, keepdims=True)
    total = jnp.sum(jnp.sum(sums, axis=0, keepdims=True), axis=1, keepdims=True)
    scale_ref[...] = jnp.where(iota((8, 128), 0) == 0, scale, total)
    inverse_ref[...] = scale / jnp.where(sums > 0.0, sums, 1.0)
    for j in range(1, CAP):

        @pl.when(j < n)
        def _(j=j):
            line = inverse_ref[j : j + 1, :]
            grown_ref[j - 1 : j, :] += level(edge[j], line)
            grown_ref[j : j + 1, :] += level(diagonal(j), line)
            below = upright(edge[j + 1], line)
            grown_ref[j + 1 : j + 2, :] += jnp.where(jnp.logical_or(j + 1 < n, last), below, 0.0)


def edge_kernel(
    c_hbm, count_hbm, row_hbm, col_hbm,
    edge, diagonal, near_ref, far_ref, first_ref, spill_ref, sums_ref, grown_ref, scale_ref, info_ref,
    count_s, row_s, col_s, last_diagonal, inverse_ref, tile_sem, int_sem, sem,
):
    me = lax.axis_index("dev")
    block = pl.ds(pl.multiple_of((me // 16) * 128, 128), 128)
    ints = [
        pltpu.make_async_copy(count_hbm.at[pl.ds(pl.multiple_of((me // 128) * 128, 128), 128)], count_s, int_sem.at[0]),
        pltpu.make_async_copy(row_hbm.at[block], row_s, int_sem.at[1]),
        pltpu.make_async_copy(col_hbm.at[block], col_s, int_sem.at[2]),
    ]
    copies = [pltpu.make_async_copy(c_hbm.at[max(2 * j - 1, 0)], edge.at[j], tile_sem.at[j]) for j in range(CAP + 1)]
    others = [
        pltpu.make_async_copy(c_hbm.at[2 * j], diagonal.at[j - 1], tile_sem.at[CAP + j]) for j in (1, 2)
    ]
    for copy in ints:
        copy.start()
    for copy in copies[:EARLY]:
        copy.start()
    others[0].start()
    for copy in ints:
        copy.wait()
    count = count_s[me % 128]
    n = (count + 1) // 2
    for j in range(EARLY, CAP + 1):

        @pl.when(2 * j - 1 < count)
        def _(j=j):
            copies[j].start()

    @pl.when(n > 2)
    def _():
        others[1].start()

    base = (me % 16) * SLOTS
    odd = me % 2
    row = [row_s[base + k] for k in range(SLOTS)]
    col = [col_s[base + k] for k in range(SLOTS)]
    start = row[0]
    for k in range(1, SLOTS):
        start = jnp.minimum(start, jnp.where(k < count, row[k], start))
    info_ref[0] = n
    info_ref[1] = count
    info_ref[2] = odd
    for j in range(2 * CAP):
        info_ref[AT_DIAG + j] = 0
    strange = jnp.int32(0)
    for k in range(SLOTS):
        held = k < count
        local_row = jnp.where(held, row[k] - start, -1)
        local_col = jnp.where(held, col[k] - start, -1)
        info_ref[AT_ROW + k] = local_row
        info_ref[AT_COL + k] = local_col
        usual = jnp.logical_and(local_row == k // 2, local_col == (k + 1) // 2)
        strange = jnp.where(jnp.logical_or(usual, jnp.logical_not(held)), strange, 1)

        @pl.when(held)
        def _(k=k, local_row=local_row, local_col=local_col):
            info_ref[jnp.where(local_row == local_col, AT_DIAG, AT_OFF) + local_row] = k

    info_ref[STRANGE] = strange

    def rest():
        for j in range(2, EARLY):

            @pl.when(j > n)
            def _(j=j):
                copies[j].wait()

        others[0].wait()

        @pl.when(n > 2)
        def _():
            others[1].wait()

        @pl.when(strange != 0)
        def _():
            for j in (1, 2):
                copy = pltpu.make_async_copy(
                    c_hbm.at[info_ref[AT_DIAG + j]], diagonal.at[j - 1], tile_sem.at[CAP + j]
                )
                copy.start()
                copy.wait()

    def first_of(part):
        return part + jnp.where(count >= 2, level_sum(edge[1]), 0.0)

    def spill_of():
        return jnp.where(count == 2 * n, upright_sum(edge[n]), 0.0)

    copies[0].wait()
    copies[1].wait()
    first_ref[...] = first_of(upright_sum(edge[0]))
    for j in range(2, CAP + 1):

        @pl.when(j <= n)
        def _(j=j):
            if j >= EARLY:
                pl.when(2 * j - 1 < count)(copies[j].wait)
            else:
                copies[j].wait()

    spill_ref[...] = spill_of()

    @pl.when(strange != 0)
    def _():
        for j in range(CAP + 1):
            slot = info_ref[AT_DIAG] if j == 0 else info_ref[AT_OFF + j - 1]
            copy = pltpu.make_async_copy(c_hbm.at[slot], edge.at[j], tile_sem.at[j])
            copy.start()
            copy.wait()
        first_ref[...] = first_of(upright_sum(edge[0]))
        spill_ref[...] = spill_of()

    near_ref[...], far_ref[...] = boundary(odd == 1, spill_ref[...], first_ref[...])
    rest()
    ahead_of_partner = jnp.logical_or(jnp.logical_and(odd == 1, me % 8 != 7), jnp.logical_and(me % 64 == 0, me > 0))
    info_ref[EARLY_BIRD] = jnp.where(ahead_of_partner, 1, 0)

    @pl.when(ahead_of_partner)
    def _():
        interior(
            info_ref, c_hbm, edge, diagonal, first_ref, spill_ref, sums_ref, grown_ref, scale_ref,
            last_diagonal, inverse_ref, sem,
        )


def middle_kernel(
    info_ref, c_hbm, edge, diagonals, first_ref, spill_ref, sums_in, grown_in, scale_in,
    sums_ref, grown_ref, scale_ref,
    last_diagonal, inverse_ref, sem,
):
    @pl.when(info_ref[EARLY_BIRD] == 0)
    def _():
        interior(
            info_ref, c_hbm, edge, diagonals, first_ref, spill_ref, sums_ref, grown_ref, scale_ref,
            last_diagonal, inverse_ref, sem,
        )


def second_kernel(
    info_ref, edge, sums_ref, grown_ref, scale_in, near_in, far_in,
    raw_ref, part_ref, near_ref, far_ref, sent_ref,
    inverse_ref,
):
    n = info_ref[0]
    count = info_ref[1]
    odd = info_ref[2] == 1
    rows = iota((ROWS, TILE), 0)
    local = sums_ref[...]
    ahead, behind = jnp.where(odd, far_in[...], near_in[...]), jnp.where(odd, near_in[...], far_in[...])
    raw = local + jnp.where(rows == 0, behind, 0.0) + jnp.where(rows == n, ahead, 0.0)
    raw = jnp.where(raw > 0.0, raw, 1.0)
    raw_ref[...] = raw
    scale = scale_in[0:1, 0:1]
    inverse = scale / raw
    inverse_ref[...] = inverse
    top = inverse_ref[0:1, :]
    next_row = inverse_ref[pl.ds(n, 1), :]
    here = level(edge[0], top)
    below = jnp.where(count >= 2, upright(edge[1], top), 0.0)
    across = jnp.where(count == 2 * n, level(edge[n], next_row), 0.0)
    grown = grown_ref[...] + jnp.where(rows == 0, here, 0.0) + jnp.where(rows == 1, below, 0.0)
    part = (grown + jnp.where(rows == n - 1, across, 0.0)) * inverse
    part_ref[...] = part
    column = jnp.sum(part, axis=0, keepdims=True)
    quarter = column[:, :128] + column[:, 128:256] + column[:, 256:384] + column[:, 384:]
    folded = jnp.broadcast_to(quarter, (8, 128))
    folded = folded + pltpu.roll(folded, 64, 1)
    sent = jnp.where(iota((8, 128), 1) < 64, scale_in[1:2, :], jnp.sqrt(folded) / scale_in[0:1, :])
    sent_ref[...] = jnp.concatenate([sent] * (DEVICES // 8), axis=0)
    spill = jnp.sum(jnp.where(rows == n, part, 0.0), axis=0, keepdims=True)
    near_ref[:, :TILE], far_ref[:, :TILE] = boundary(odd, spill, part[0:1, :])
    near_ref[:, TILE:] = scale_in[0:1, :]
    far_ref[:, TILE:] = scale_in[0:1, :]


def factor_kernel(
    info_ref, c_hbm, raw_ref, part_ref, scale_ref, near_in, far_in,
    tiles, weight_ref, row_factor_ref, col_factor_ref, out_hbm, zeros, sem, zero_sem,
):
    copy = pltpu.make_async_copy(c_hbm.at[pl.ds(0, KEPT)], tiles, sem)
    copy.start()
    n = info_ref[0]
    count = info_ref[1]
    zeros[...] = jnp.zeros((TILE, TILE), BF16)
    blanks = [None] + [pltpu.make_async_copy(zeros, out_hbm.at[k], zero_sem.at[k]) for k in range(1, SLOTS)]
    for k in range(1, SLOTS):

        @pl.when(k >= count)
        def _(k=k):
            blanks[k].start()

    odd = info_ref[2] == 1
    rows = iota((ROWS, TILE), 0)
    scale = jnp.concatenate([scale_ref[0:1, :]] * 4, axis=1)
    ahead = jnp.where(odd, far_in[...], near_in[...])
    behind = jnp.where(odd, near_in[...], far_in[...])

    def rescaled(x):
        other = jnp.concatenate([x[:, TILE:]] * 4, axis=1)
        ratio = jnp.where(other > 0.0, scale / jnp.where(other > 0.0, other, 1.0), 0.0)
        return x[:, :TILE] * ratio * ratio

    part = part_ref[...] + jnp.where(rows == 0, rescaled(behind), 0.0) + jnp.where(rows == n, rescaled(ahead), 0.0)
    weight = raw_ref[...] / scale * part
    weight = jnp.where(weight > 0.0, weight, 1.0)
    weight_ref[...] = weight
    inverse = 1.0 / weight
    slots = iota((SLOTS, TILE), 0)
    col_at = jnp.full((SLOTS, TILE), -1, jnp.int32)
    for k in range(SLOTS):
        col_at = jnp.where(slots == k, info_ref[AT_COL + k], col_at)
    col_factor_ref[...] = gather(inverse, col_at)
    row_factor_ref[...] = jnp.transpose(inverse)
    copy.wait()
    for k in range(1, SLOTS):

        @pl.when(k >= count)
        def _(k=k):
            blanks[k].wait()


def last_kernel(
    info_ref, all_ref, c_hbm, kept, raw_ref, weight_ref, scale_ref, row_factor_ref, col_factor_ref, blank_hbm,
    one_hbm, two_hbm, out_hbm, tiles, buffer, one_ref, two_ref, columns_ref, rows_ref, in_sem, sem, bias_sem,
):
    n = info_ref[0]
    count = info_ref[1]
    copies = [pltpu.make_async_copy(c_hbm.at[k], tiles.at[k - KEPT], in_sem.at[k - KEPT]) for k in range(KEPT, SLOTS)]
    for k in range(KEPT, SLOTS):

        @pl.when(k < count)
        def _(k=k):
            copies[k - KEPT].start()


    def send(k, half):
        part = pl.ds(half * TILE // HALVES, TILE // HALVES)
        return pltpu.make_async_copy(buffer.at[k, part], out_hbm.at[k, part], sem.at[k, half])

    def broadcast_row(j):
        rows_ref[j] = jnp.broadcast_to(row_factor_ref[:, j : j + 1], (TILE, 128))

    @pl.when(info_ref[STRANGE] != 0)
    def _():
        for j in range(1, CAP):
            broadcast_row(j)

    broadcast_row(0)
    lanes = iota((1, 128), 1)
    everyone = all_ref[...]
    scale = scale_ref[0:1, 0:1]
    scaled = everyone * scale_ref[0:1, :]
    total_one = jnp.sum(everyone, axis=0, keepdims=True)
    total_two = jnp.sum(scaled * scaled, axis=0, keepdims=True)
    mean_one = jnp.sum(jnp.where(lanes == 0, total_one, 0.0), axis=1, keepdims=True) / BINS
    sum_two = jnp.sum(jnp.where(lanes >= 64, total_two, 0.0), axis=1, keepdims=True)
    unit = (sum_two / BINS) * (mean_one / scale)
    columns_ref[...] = col_factor_ref[...] * unit * unit * TILE
    one = raw_ref[...] / mean_one
    two = weight_ref[...] / unit
    for j in range(CAP):
        one_ref[:, j * TILE : (j + 1) * TILE] = jnp.where(j < n, one[j : j + 1, :], 0.0)
        two_ref[:, j * TILE : (j + 1) * TILE] = jnp.where(j < n, two[j : j + 1, :], 0.0)
    biases = [
        pltpu.make_async_copy(one_ref, one_hbm, bias_sem.at[0]),
        pltpu.make_async_copy(two_ref, two_hbm, bias_sem.at[1]),
    ]
    for copy in biases:
        copy.start()
    for k in range(SLOTS):

        @pl.when(k < count)
        def _(k=k):
            if k > 0 and k % 2 == 0:
                broadcast_row(k // 2)
            if k >= KEPT:
                copies[k - KEPT].wait()
                tile = tiles[k - KEPT]
            else:
                tile = kept[k]
            row = jnp.concatenate([rows_ref[info_ref[AT_ROW + k]]] * 4, axis=1)
            columns = columns_ref[k : k + 1, :]
            for half in range(HALVES):
                part = slice(half * TILE // HALVES, (half + 1) * TILE // HALVES)
                buffer[k, part] = (tile[part].astype(F32) * row[part] * columns).astype(BF16)
                send(k, half).start()

    for copy in biases:
        copy.wait()
    for k in range(SLOTS):

        @pl.when(k < count)
        def _(k=k):
            for half in range(HALVES):
                send(k, half).wait()


VMEM = pl.BlockSpec(memory_space=pltpu.VMEM)
SMEM = pl.BlockSpec(memory_space=pltpu.SMEM)
HBM = pl.BlockSpec(memory_space=pltpu.HBM)


def in_hbm(x):
    return pltpu.with_memory_space_constraint(x, pltpu.HBM)


def shards(contacts, tile_count, tile_row, tile_col, range_rows):
    near_pairs = [(i, i ^ 1) for i in range(DEVICES)]
    far_pairs = [(i, ((i + 1) ^ 1) - 1) for i in range(1, DEVICES - 1)]
    window = pltpu.VMEM((ROWS, TILE), F32)
    line = pltpu.VMEM((1, TILE), F32)
    long = pltpu.VMEM((1, TILE + 128), F32)
    splat = pltpu.VMEM((8, 128), F32)
    edge, diagonal, near, far, first, spill, sums, grown, scale, info = pl.pallas_call(
        edge_kernel,
        out_shape=(
            pltpu.VMEM((CAP + 1, TILE, TILE), BF16), pltpu.VMEM((2, TILE, TILE), BF16), line, line, line, line,
            window, window, splat, pltpu.SMEM((INFO,), jnp.int32),
        ),
        in_specs=[HBM] * 4,
        out_specs=(VMEM,) * 9 + (SMEM,),
        scratch_shapes=[
            pltpu.SMEM((128,), jnp.int32),
            pltpu.SMEM((128,), jnp.int32),
            pltpu.SMEM((128,), jnp.int32),
            pltpu.VMEM((TILE, TILE), BF16),
            window,
            pltpu.SemaphoreType.DMA((CAP + 3,)),
            pltpu.SemaphoreType.DMA((3,)),
            pltpu.SemaphoreType.DMA,
        ],
        compiler_params=pltpu.CompilerParams(vmem_limit_bytes=24 << 20),
        name="edge",
    )(*(in_hbm(x) for x in (contacts, tile_count, tile_row, tile_col)))
    far = lax.ppermute(far, "dev", far_pairs)
    near = lax.ppermute(near, "dev", near_pairs)
    sums, grown, scale = pl.pallas_call(
        middle_kernel,
        out_shape=(window, window, splat),
        in_specs=[SMEM, HBM] + [VMEM] * 7,
        out_specs=(VMEM,) * 3,
        input_output_aliases={6: 0, 7: 1, 8: 2},
        scratch_shapes=[
            pltpu.VMEM((TILE, TILE), BF16),
            window,
            pltpu.SemaphoreType.DMA,
        ],
        compiler_params=pltpu.CompilerParams(vmem_limit_bytes=24 << 20),
        name="middle",
    )(info, in_hbm(contacts), edge, diagonal, first, spill, sums, grown, scale)
    raw, part, near, far, sent = pl.pallas_call(
        second_kernel,
        out_shape=(window, window, long, long, pltpu.VMEM((DEVICES, 128), F32)),
        in_specs=[SMEM] + [VMEM] * 6,
        out_specs=(VMEM,) * 5,
        scratch_shapes=[window],
        compiler_params=pltpu.CompilerParams(vmem_limit_bytes=24 << 20),
        name="second",
    )(info, edge, sums, grown, scale, near, far)
    far = lax.ppermute(far, "dev", far_pairs)
    near = lax.ppermute(near, "dev", near_pairs)
    everyone = lax.all_to_all(sent, "dev", 0, 0, tiled=True)
    balanced = jax.ShapeDtypeStruct((SLOTS, TILE, TILE), BF16)
    tiles, weight, row_factor, col_factor, blank = pl.pallas_call(
        factor_kernel,
        out_shape=(pltpu.VMEM((KEPT, TILE, TILE), BF16), window, pltpu.VMEM((TILE, SLOTS), F32), window, balanced),
        in_specs=[SMEM, HBM] + [VMEM] * 5,
        out_specs=(VMEM,) * 4 + (HBM,),
        scratch_shapes=[
            pltpu.VMEM((TILE, TILE), BF16), pltpu.SemaphoreType.DMA, pltpu.SemaphoreType.DMA((SLOTS,)),
        ],
        compiler_params=pltpu.CompilerParams(vmem_limit_bytes=24 << 20),
        name="factor",
    )(info, in_hbm(contacts), raw, part, scale, near, far)
    return pl.pallas_call(
        last_kernel,
        out_shape=(
            jax.ShapeDtypeStruct((1, CAP * TILE), F32),
            jax.ShapeDtypeStruct((1, CAP * TILE), F32),
            balanced,
        ),
        in_specs=[SMEM, VMEM, HBM] + [VMEM] * 6 + [HBM],
        out_specs=(HBM,) * 3,
        input_output_aliases={9: 2},
        scratch_shapes=[
            pltpu.VMEM((SLOTS - KEPT, TILE, TILE), BF16),
            pltpu.VMEM((SLOTS, TILE, TILE), BF16),
            pltpu.VMEM((1, CAP * TILE), F32),
            pltpu.VMEM((1, CAP * TILE), F32),
            window,
            pltpu.VMEM((CAP, TILE, 128), F32),
            pltpu.SemaphoreType.DMA((SLOTS - KEPT,)),
            pltpu.SemaphoreType.DMA((SLOTS, HALVES)),
            pltpu.SemaphoreType.DMA((2,)),
        ],
        compiler_params=pltpu.CompilerParams(vmem_limit_bytes=32 << 20),
        name="last",
    )(info, everyone, in_hbm(contacts), tiles, raw, weight, scale, row_factor, col_factor, blank)


def solution(mesh):
    return jax.shard_map(
        shards,
        mesh=mesh,
        in_specs=(P("dev", None, None), P(), P(), P(), P()),
        out_specs=(P("dev", None), P("dev", None), P("dev", None, None)),
        check_vma=False,
    )
```
